128 devices in a mesh: det: 16 (over z_lo, x, core), strip: 8 (over y, z_hi).
Axes of the slice: x: 4, y: 4, z: 4 (z_hi: 2, z_lo: 2; z = z_hi * 2 + z_lo), core: 2. Of those that a mesh axis runs over, the one named last changes fastest.
Arguments:
- science: float32 [16, 256, 4096], P('det', 'strip'), may hold values from -17 to 17
- template: float32 [16, 256, 4096], P(None, 'strip', 'det'), may hold values from -8 to 8
- row_taps: float32 [12, 21], replicated, may hold values from -1.25 to 1.25
- col_taps: float32 [12, 21], replicated, may hold values from -1.25 to 1.25
- stamp_rows: int32 [16, 32], P('det'), may hold values from 17 to 238
- stamp_cols: int32 [16, 32], P('det'), may hold values from 17 to 4078
Outputs:
- difference: float32 [16, 256, 4096], P('det', 'strip')
- kernel_coeffs: float32 [16, 37], P('det')
The draws below stay inside these ranges and needn't reach their ends.
All inputs are finite; a program needn't handle non-finite values.
Results may differ from the reference program's by a relative error of at most 0.0003.
Values sent between devices are 32-bit elements; how exact they have to be, the bound alone decides.
A program may use at most 128 MiB of HBM per device.

```python
import jax
import jax.numpy as jnp
from jax import lax

COLS = 4096
NB = 12
KS = 21
HS = 17
NSTAMP = 32
KH = 10
NU = 37
DETS = 16
ROWS = 256


def sky_pair(key):
    shape = (DETS, ROWS, COLS)
    rough = jnp.clip(jax.random.normal(jax.random.fold_in(key, 11), shape, jnp.float32), -6.0, 6.0)
    template = rough
    offsets = 0.3 + 0.6 * jax.random.uniform(jax.random.fold_in(key, 13), (DETS, 1, 1), jnp.float32)
    noise = jnp.clip(jax.random.normal(jax.random.fold_in(key, 14), shape, jnp.float32), -6.0, 6.0)
    x_coord = (2.0 * jnp.arange(COLS, dtype=jnp.float32) / COLS - 1.0)[None, None, :]
    science = offsets + (0.7 + 0.3 * x_coord) * template + 0.3 * jnp.roll(template, 1, axis=2) + 0.2 * jnp.roll(template, -1, axis=1) + 0.5 * noise
    return (science, template)


def draw_science(key, part):
    return sky_pair(key)[0]


def draw_template(key, part):
    return sky_pair(key)[1]


def touch_ends(entries, rng, low, largest):
    extent = entries.shape
    index_at = [jax.random.randint(jax.random.fold_in(rng, axis), (), 0, extent[axis]) for axis in range(len(extent))]
    entries = entries.at[tuple(index_at)].set(low)
    longest = extent.index(max(extent))
    index_at[longest] = (index_at[longest] + 1) % extent[longest]
    return entries.at[tuple(index_at)].set(largest)


def centred(stream_key, extent, deviation, reach, held_as=jnp.bfloat16):
    return jnp.clip(deviation * jax.random.normal(stream_key, extent, jnp.float32), -reach, reach).astype(held_as)


def setup_inputs(seed: int = 0) -> dict:
    splits = jax.random.split(jax.random.key(seed), 7)
    science = draw_science(jax.random.fold_in(splits[6], 71), 0)
    template = draw_template(jax.random.fold_in(splits[6], 71), 0)
    row_taps = centred(splits[2], (NB, KS), KS ** -0.5, 1.25, jnp.float32)
    col_taps = centred(splits[3], (NB, KS), KS ** -0.5, 1.25, jnp.float32)
    stamp_rows = touch_ends(jax.random.randint(splits[4], (DETS, NSTAMP), HS, ROWS - HS), jax.random.fold_in(splits[4], 1), HS, (ROWS - HS) - 1).astype(jnp.int32)
    stamp_cols = touch_ends(jax.random.randint(splits[5], (DETS, NSTAMP), HS, COLS - HS), jax.random.fold_in(splits[5], 1), HS, (COLS - HS) - 1).astype(jnp.int32)
    return {"science": science, "template": template, "row_taps": row_taps, "col_taps": col_taps, "stamp_rows": stamp_rows, "stamp_cols": stamp_cols}


RIDGE_WEIGHT = 1.0
HIGHEST_MODE = lax.Precision.HIGHEST

def correlate(picture, row_taps, col_taps):
    planes = picture[None, None]
    across = lax.conv_general_dilated(planes, col_taps[:, None, None, :], (1, 1), ((0, 0), (KH, KH)), precision=HIGHEST_MODE)
    return lax.conv_general_dilated(across, row_taps[:, None, :, None], (1, 1), ((KH, KH), (0, 0)), feature_group_count=NB, precision=HIGHEST_MODE)[0]

def features(responses, y_coord, x_coord):
    flat = responses.reshape(NB, -1)
    y_flat = jnp.broadcast_to(y_coord, responses.shape[1:]).reshape(1, -1)
    x_flat = jnp.broadcast_to(x_coord, responses.shape[1:]).reshape(1, -1)
    unity = jnp.ones((1, flat.shape[1]), jnp.float32)
    return jnp.concatenate([flat, flat * x_flat, flat * y_flat, unity], axis=0)

def apply_model(responses, coeffs, y_coord, x_coord):
    base_part = jnp.tensordot(coeffs[:NB], responses, axes=1, precision=HIGHEST_MODE)
    x_part = jnp.tensordot(coeffs[NB:2 * NB], responses, axes=1, precision=HIGHEST_MODE)
    y_part = jnp.tensordot(coeffs[2 * NB:3 * NB], responses, axes=1, precision=HIGHEST_MODE)
    return base_part + x_coord * x_part + y_coord * y_part + coeffs[NU - 1]

def reference(science, template, row_taps, col_taps, stamp_rows, stamp_cols):
    y_coord = (2.0 * jnp.arange(ROWS, dtype=jnp.float32) / ROWS - 1.0)[:, None]
    x_coord = (2.0 * jnp.arange(COLS, dtype=jnp.float32) / COLS - 1.0)[None, :]
    stamp_side = 2 * HS + 1

    def one_detector(inputs):
        picture, observed, rows_at, cols_at = inputs
        responses = correlate(picture, row_taps, col_taps)

        def one_stamp(centre):
            top_row = (centre[0] - HS).astype(jnp.int32)
            left_col = (centre[1] - HS).astype(jnp.int32)
            anchor = jnp.zeros((), jnp.int32)
            window = lax.dynamic_slice(responses, (anchor, top_row, left_col), (NB, stamp_side, stamp_side))
            y_window = lax.dynamic_slice(y_coord, (top_row, anchor), (stamp_side, 1))
            x_window = lax.dynamic_slice(x_coord, (anchor, left_col), (1, stamp_side))
            sci_window = lax.dynamic_slice(observed, (top_row, left_col), (stamp_side, stamp_side))
            feats = features(window, y_window, x_window)
            normal = jnp.dot(feats.astype(jnp.float32), feats.T.astype(jnp.float32), precision=HIGHEST_MODE, preferred_element_type=jnp.float32)
            target = jnp.dot(feats.astype(jnp.float32), sci_window.reshape(-1).astype(jnp.float32), precision=HIGHEST_MODE, preferred_element_type=jnp.float32)
            return (normal, target)
        normals, targets = lax.map(one_stamp, jnp.stack([rows_at, cols_at], axis=1))
        normal = jnp.sum(normals, axis=0) + RIDGE_WEIGHT * jnp.eye(NU, dtype=jnp.float32)
        coeffs = jnp.linalg.solve(normal, jnp.sum(targets, axis=0))
        return (observed - apply_model(responses, coeffs, y_coord, x_coord), coeffs)
    difference, kernel_coeffs = lax.map(one_detector, (template, science, stamp_rows, stamp_cols))
    return (difference, kernel_coeffs)
```

```python
import jax
import jax.numpy as jnp
from jax import lax
from jax.experimental import pallas as pl
from jax.experimental.pallas import tpu as pltpu
from jax.sharding import PartitionSpec as P

NB = 12
KS = 21
HS = 17
KH = 10
NU = 37
NSTAMP = 32
LANE = 128
HALO = 16
FEAT = 16
GRAM = 3 * FEAT
MESH = pl.DeviceIdType.MESH
F32 = jnp.float32
BF16 = jnp.bfloat16


def halves(value):
    high = value.astype(BF16)
    return high, (value - high.astype(F32)).astype(BF16)


def model_kernel(rows, tiles, strips, ext_ref, sci_ref, rtap_ref, ctap_ref, srow_ref, scol_ref,
                 resp_ref, gram_ref, taps, frame, v_hi, v_lo, held, weight, flags, feat, acc):
    b = pl.program_id(0)
    depth = rows + 2 * HALO
    strip = lax.axis_index("strip")
    groups = rows // 8

    @pl.when(b == 0)
    def _():
        taps[...] = jnp.zeros_like(taps)
        taps[0:NB, 0:KS] = rtap_ref[...]
        parts = []
        for n in range(NB):
            row = jnp.broadcast_to(taps[n : n + 1, 0:LANE], (rows, LANE))
            parts.append(pltpu.roll(row, HALO - KH, 1, stride=1, stride_axis=0))
        table = jnp.concatenate(parts, axis=0)
        table = table + pltpu.roll(table, depth, 1)
        t_hi, t_lo = halves(table)
        left = jnp.concatenate([t_hi, t_lo], axis=1)
        taps[0:NB, 0:KS] = ctap_ref[...]

        grow = strip * rows - HALO + lax.broadcasted_iota(jnp.int32, (depth, 1), 0)
        inside = jnp.logical_and(grow >= 0, grow < strips * rows)
        whole = jnp.where(inside, ext_ref[...], 0.0)
        whole = jnp.concatenate([whole, jnp.zeros((depth, 2 * LANE), F32)], axis=1)
        whole = pltpu.roll(whole, KH, 1)
        f_hi, f_lo = halves(whole)
        both = jnp.concatenate([f_hi, f_lo, f_hi, f_lo], axis=0)
        for k in range(tiles // 2 + 1):
            frame[k] = both[:, 2 * LANE * k : 2 * LANE * (k + 1)]

        def down(k, carry):
            out = jnp.dot(left, frame[k], preferred_element_type=F32)
            o_hi, o_lo = halves(out)
            for n in range(NB):
                for side in range(2):
                    at = pl.ds(pl.multiple_of((2 * k + side) * rows, rows), rows)
                    piece = (slice(n * rows, (n + 1) * rows), slice(side * LANE, (side + 1) * LANE))
                    v_hi[n, at, :] = o_hi[piece]
                    v_lo[n, at, :] = o_lo[piece]
            return carry

        lax.fori_loop(0, tiles // 2 + 1, down, 0)

    band = pltpu.roll(
        jnp.broadcast_to(taps[pl.ds(b, 1), :], (LANE, 2 * LANE)), 0, 1, stride=1, stride_axis=0
    )
    b_hi, b_lo = halves(band)
    span = tiles * rows
    a_hi = jnp.concatenate([v_hi[b, 0:span, :], v_hi[b, rows : span + rows, :]], axis=1)
    a_lo = jnp.concatenate([v_lo[b, 0:span, :], v_lo[b, rows : span + rows, :]], axis=1)
    out = lax.dot_general(
        jnp.concatenate([a_hi, a_lo, a_hi], axis=1),
        jnp.concatenate([b_hi, b_hi, b_lo], axis=1),
        (((1,), (1,)), ((), ())),
        preferred_element_type=F32,
    )
    resp_ref[0] = out
    held[b] = out

    @pl.when(b == NB - 1)
    def _():
        weight[...] = jnp.zeros_like(weight)
        acc[...] = jnp.zeros_like(acc)
        for p in range(8):
            feat[p * FEAT : (p + 1) * FEAT, :] = jnp.where(
                lax.broadcasted_iota(jnp.int32, (FEAT, LANE), 0) == NB, 1.0, 0.0
            )

        def clear(t, carry):
            flags[t] = 0
            return carry

        lax.fori_loop(0, tiles, clear, 0)
        first = strip * rows
        row_id = lax.broadcasted_iota(jnp.int32, (rows, LANE), 0)
        col_id = lax.broadcasted_iota(jnp.int32, (rows, LANE), 1)

        def mark(s, carry):
            top = srow_ref[0, s] - HS - first
            end = srow_ref[0, s] + HS - first
            left = scol_ref[0, s] - HS
            right = scol_ref[0, s] + HS

            @pl.when(jnp.logical_and(end >= 0, top < rows))
            def _():
                low = lax.shift_right_logical(jnp.maximum(top, 0), 3)
                high = lax.shift_right_logical(jnp.minimum(end, rows - 1), 3)
                bits = lax.shift_left(2, high) - lax.shift_left(1, low)
                in_row = jnp.logical_and(row_id >= top, row_id <= end)
                t0 = lax.shift_right_logical(left, 7)
                t1 = lax.shift_right_logical(right, 7)

                def tile(t, carry):
                    flags[t] = flags[t] | bits
                    col = col_id + t * LANE
                    hit = jnp.logical_and(in_row, jnp.logical_and(col >= left, col <= right))
                    at = pl.ds(pl.multiple_of(t * rows, rows), rows)
                    weight[at, :] += hit.astype(F32)
                    return carry

                lax.fori_loop(t0, t1 + 1, tile, 0)

            return carry

        lax.fori_loop(0, NSTAMP, mark, 0)

        sub = lax.broadcasted_iota(jnp.int32, (8, FEAT, LANE), 0)
        lane = lax.broadcasted_iota(jnp.int32, (1, 1, LANE), 2)

        def unit(t, carry):
            mask = flags[t]
            x_coord = 2.0 * (t * LANE + lane).astype(F32) / (tiles * LANE) - 1.0
            for g in range(groups):

                @pl.when((mask & (1 << g)) != 0)
                def _():
                    at = pl.ds(pl.multiple_of(t * rows + g * 8, 8), 8)
                    for n in range(NB):
                        feat[pl.ds(n, 8, stride=FEAT), :] = held[n, at, :]
                    cols = pl.ds(pl.multiple_of(t * LANE, LANE), LANE)
                    feat[pl.ds(NB + 1, 8, stride=FEAT), :] = sci_ref[g * 8 : (g + 1) * 8, cols]
                    base = feat[...].reshape(8, FEAT, LANE)
                    y_coord = 2.0 * (first + g * 8 + sub).astype(F32) / (strips * rows) - 1.0
                    hits = weight[at, :]
                    plain = (base, base * x_coord, base * y_coord)
                    l_parts, r_parts = [], []
                    for p in range(8):
                        wp = hits[p : p + 1, :]
                        stack = jnp.concatenate([f[p] for f in plain], axis=0)
                        r_hi, r_lo = halves(stack)
                        w_hi, w_lo = halves(stack * wp)
                        r_parts.append(jnp.concatenate([r_hi, r_lo], axis=0))
                        l_parts.append(jnp.concatenate([w_hi, w_lo], axis=0))
                    acc[:, 0 : 2 * GRAM] += lax.dot_general(
                        jnp.concatenate(l_parts, axis=1),
                        jnp.concatenate(r_parts, axis=1),
                        (((1,), (1,)), ((), ())),
                        preferred_element_type=F32,
                    )

            return carry

        lax.fori_loop(0, tiles, unit, 0)
        total = acc[...]
        total = total + pltpu.roll(total, LANE - GRAM, 1)
        gram_ref[...] = total[0:GRAM] + total[GRAM : 2 * GRAM]


def model(ext, science, row_taps, col_taps, stamp_rows, stamp_cols, strips):
    rows, cols = science.shape
    tiles = cols // LANE
    whole = lambda shape: pl.BlockSpec(shape, lambda b: (0,) * len(shape))
    return pl.pallas_call(
        lambda *refs: model_kernel(rows, tiles, strips, *refs),
        grid=(NB,),
        in_specs=[
            whole(ext.shape),
            whole(science.shape),
            whole(row_taps.shape),
            whole(col_taps.shape),
            pl.BlockSpec(memory_space=pltpu.SMEM),
            pl.BlockSpec(memory_space=pltpu.SMEM),
        ],
        out_specs=[
            pl.BlockSpec((1, tiles * rows, LANE), lambda b: (b, 0, 0)),
            whole((GRAM, LANE)),
        ],
        out_shape=[
            jax.ShapeDtypeStruct((NB, tiles * rows, LANE), F32),
            jax.ShapeDtypeStruct((GRAM, LANE), F32),
        ],
        scratch_shapes=[
            pltpu.VMEM((16, 2 * LANE), F32),
            pltpu.VMEM((tiles // 2 + 1, 4 * (rows + 2 * HALO), 2 * LANE), BF16),
            pltpu.VMEM((NB, (tiles + 2) * rows, LANE), BF16),
            pltpu.VMEM((NB, (tiles + 2) * rows, LANE), BF16),
            pltpu.VMEM((NB, tiles * rows, LANE), F32),
            pltpu.VMEM((tiles * rows, LANE), F32),
            pltpu.SMEM((tiles,), jnp.int32),
            pltpu.VMEM((8 * FEAT, LANE), F32),
            pltpu.VMEM((2 * GRAM, LANE), F32),
        ],
        compiler_params=pltpu.CompilerParams(vmem_limit_bytes=48 * 1024 * 1024),
        name="model",
    )(ext, science, row_taps, col_taps, stamp_rows, stamp_cols)


def reduce_kernel(strips, part_ref, total_ref, slots, send_sem, recv_sem):
    me = lax.axis_index("strip")
    barrier = pltpu.get_barrier_semaphore()
    for k in range(1, strips):
        peer = lax.rem(me + k, strips)
        pl.semaphore_signal(barrier, inc=1, device_id={"strip": peer}, device_id_type=MESH)
    pl.semaphore_wait(barrier, strips - 1)
    copies = []
    for k in range(1, strips):
        peer = lax.rem(me + k, strips)
        copy = pltpu.make_async_remote_copy(
            src_ref=part_ref,
            dst_ref=slots.at[me],
            send_sem=send_sem.at[k],
            recv_sem=recv_sem.at[me],
            device_id={"strip": peer},
            device_id_type=MESH,
        )
        copy.start()
        copies.append(copy)
    slots[me] = part_ref[...]
    for k in range(1, strips):
        source = lax.rem(me + k, strips)
        pltpu.make_async_remote_copy(
            src_ref=part_ref,
            dst_ref=slots.at[source],
            send_sem=send_sem.at[k],
            recv_sem=recv_sem.at[source],
            device_id={"strip": source},
            device_id_type=MESH,
        ).wait_recv()
    total = slots[0]
    for s in range(1, strips):
        total = total + slots[s]
    total_ref[...] = total
    for copy in copies:
        copy.wait_send()


def reduce(part, strips):
    return pl.pallas_call(
        lambda *refs: reduce_kernel(strips, *refs),
        out_shape=jax.ShapeDtypeStruct(part.shape, F32),
        in_specs=[pl.BlockSpec(memory_space=pltpu.VMEM)],
        out_specs=pl.BlockSpec(memory_space=pltpu.VMEM),
        scratch_shapes=[
            pltpu.VMEM((strips,) + part.shape, F32),
            pltpu.SemaphoreType.DMA((strips,)),
            pltpu.SemaphoreType.DMA((strips,)),
        ],
        compiler_params=pltpu.CompilerParams(collective_id=1, has_side_effects=True),
        name="reduce",
    )(part)


def known(index):
    return jnp.logical_or((index % FEAT) < NB, index == NB)


def apply_kernel(rows, tiles, step_tiles, strips, gram_ref, resp_ref, sci_ref, diff_ref, coef_ref, sol):
    step = pl.program_id(0)
    strip = lax.axis_index("strip")

    @pl.when(step == 0)
    def _():
        gram = gram_ref[...]
        row = lax.broadcasted_iota(jnp.int32, (GRAM, LANE), 0)
        lane = lax.broadcasted_iota(jnp.int32, (GRAM, LANE), 1)
        right = jnp.sum(jnp.where(lane == NB + 1, gram, 0.0), axis=1, keepdims=True)
        live = jnp.logical_and(known(row), jnp.logical_and(known(lane), lane < GRAM))
        system = jnp.where(live, gram, 0.0) + (row == lane).astype(F32)
        system = jnp.where(jnp.logical_and(lane == 2 * FEAT * 2, known(row)), right, system)
        for j in range(GRAM):
            if not (j % FEAT < NB or j == NB):
                continue
            column = jnp.broadcast_to(system[:, j : j + 1], (GRAM, LANE))
            pivot_row = system[j : j + 1, :] / column[j : j + 1, :]
            system = jnp.where(row == j, pivot_row, system - column * pivot_row)
        answer = jnp.broadcast_to(system[:, 4 * FEAT : 4 * FEAT + 1], (GRAM, LANE))
        sol[...] = answer
        spread = jnp.sum(jnp.where(row == lane, answer, 0.0), axis=0, keepdims=True)
        at = lax.broadcasted_iota(jnp.int32, (1, LANE), 1)
        gap = FEAT - NB
        packed = jnp.where(
            at < NB,
            spread,
            jnp.where(
                at < 2 * NB,
                pltpu.roll(spread, LANE - gap, 1),
                jnp.where(at < 3 * NB, pltpu.roll(spread, LANE - 2 * gap, 1), pltpu.roll(spread, 2 * NB, 1)),
            ),
        )
        coef_ref[...] = packed[:, 0:NU]

    lane = lax.broadcasted_iota(jnp.int32, (8, LANE), 1)
    sub = lax.broadcasted_iota(jnp.int32, (8, LANE), 0)
    for g in range(rows // 8):
        y_coord = 2.0 * (strip * rows + g * 8 + sub).astype(F32) / (strips * rows) - 1.0
        plain = [
            sol[pl.ds(n, 8, stride=0), :] + y_coord * sol[pl.ds(2 * FEAT + n, 8, stride=0), :]
            for n in range(NB)
        ]
        slope = [sol[pl.ds(FEAT + n, 8, stride=0), :] for n in range(NB)]
        offset = sol[pl.ds(NB, 8, stride=0), :]
        for t in range(step_tiles):
            col = (step * step_tiles + t) * LANE + lane
            x_coord = 2.0 * col.astype(F32) / (tiles * LANE) - 1.0
            at = slice(t * rows + g * 8, t * rows + g * 8 + 8)
            flat, tilt = offset, 0.0
            for n in range(NB):
                resp = resp_ref[n, at, :]
                flat = flat + plain[n] * resp
                tilt = tilt + slope[n] * resp
            here = (slice(g * 8, g * 8 + 8), slice(t * LANE, (t + 1) * LANE))
            diff_ref[here] = sci_ref[here] - (flat + x_coord * tilt)


def apply(gram, resp, science, strips):
    rows, cols = science.shape
    tiles = cols // LANE
    step_tiles = 4
    return pl.pallas_call(
        lambda *refs: apply_kernel(rows, tiles, step_tiles, strips, *refs),
        grid=(tiles // step_tiles,),
        in_specs=[
            pl.BlockSpec((GRAM, LANE), lambda i: (0, 0)),
            pl.BlockSpec((NB, step_tiles * rows, LANE), lambda i: (0, i, 0)),
            pl.BlockSpec((rows, step_tiles * LANE), lambda i: (0, i)),
        ],
        out_specs=[
            pl.BlockSpec((rows, step_tiles * LANE), lambda i: (0, i)),
            pl.BlockSpec((1, NU), lambda i: (0, 0)),
        ],
        out_shape=[
            jax.ShapeDtypeStruct((rows, cols), F32),
            jax.ShapeDtypeStruct((1, NU), F32),
        ],
        scratch_shapes=[pltpu.VMEM((GRAM, LANE), F32)],
        compiler_params=pltpu.CompilerParams(vmem_limit_bytes=32 * 1024 * 1024),
        name="apply",
    )(gram, resp, science)


def gather_frame(template):
    moved = lax.all_to_all(template, "det", split_axis=0, concat_axis=2, tiled=True)[0]
    strips = lax.axis_size("strip")
    forward = [(i, i + 1) for i in range(strips - 1)]
    backward = [(i + 1, i) for i in range(strips - 1)]
    low = lax.ppermute(moved[-HALO:], "strip", forward)
    high = lax.ppermute(moved[:HALO], "strip", backward)
    return jnp.concatenate([low, moved, high], axis=0)


def local(science, template, row_taps, col_taps, stamp_rows, stamp_cols):
    strips = lax.axis_size("strip")
    ext = gather_frame(template)
    resp, gram = model(ext, science[0], row_taps, col_taps, stamp_rows, stamp_cols, strips)
    gram = reduce(gram, strips)
    diff, coeffs = apply(gram, resp, science[0], strips)
    return diff[None], coeffs


def solution(mesh):
    return jax.shard_map(
        local,
        mesh=mesh,
        in_specs=(
            P("det", "strip", None),
            P(None, "strip", "det"),
            P(),
            P(),
            P("det", None),
            P("det", None),
        ),
        out_specs=(P("det", "strip", None), P("det", None)),
        check_vma=False,
    )
```
